256 devices in a mesh: tile: 64 (over z, x, core), samp: 4 (over y).
Axes of the slice: x: 4, y: 4, z: 8, core: 2. Of those that a mesh axis runs over, the one named last changes fastest.
Arguments:
- samples_w: bfloat16 [65536, 1024], P('tile', 'samp'), may hold values from -6 to 6
- dense_tiles: bfloat16 [65536, 1024], P(('tile', 'samp')), may hold values from -0.1875 to 0.1875
- left_factors: bfloat16 [65536, 2048], P('tile'), may hold values from -0.125 to 0.125
- right_factors: bfloat16 [65536, 2048], P('tile'), may hold values from -0.1875 to 0.1875
- ranks: int32 [64, 64], P(None, 'tile'), may hold values from 8 to 32
- area_blocks: bfloat16 [65536, 1024], P('tile'), may hold values from -0.03125 to 0.03125
- area_group: int32 [64], P('tile'), may hold values from 0 to 1
- counts: int32 [2048], replicated, may hold values from 0 to 5
Outputs:
- area_grad: bfloat16 [2048, 1024], P('tile', 'samp')
- sample_grad: bfloat16 [65536, 1024], P('tile', 'samp')
The draws below stay inside these ranges and needn't reach their ends.
All inputs are finite; a program needn't handle non-finite values.
Results may differ from the reference program's by a relative error of at most 0.012.
Values may be sent and summed in bfloat16 or wider, within the bound.
No kernel may reach another device: no remote copies, remote signals or barrier semaphores. Data moves between devices by JAX's collectives and lax.ppermute only.
A program may use at most 64 MiB of HBM per device.

```python
import jax
import jax.numpy as jnp
from jax import lax

B = 1024
R = 32
AREAS = 1024
GROUPS = 2
TILES = 64
CELLS = 65536
SAMPLES = 1024


def plant(entries, own_key, low, top_value):
    longest = entries.shape.index(max(entries.shape))
    spots = []
    for shift in (0, 1):
        where = [jax.random.randint(jax.random.fold_in(own_key, axis), (), 0, length) for axis, length in enumerate(entries.shape)]
        where[longest] = (where[longest] + shift) % entries.shape[longest]
        spots.append(tuple(where))
    return entries.at[spots[0]].set(low).at[spots[1]].set(top_value)


def shard_levels(own_key, shape, split, low, high):
    def one(axis_at, shards_of):
        steps = jax.random.uniform(jax.random.fold_in(jax.random.fold_in(own_key, 6), axis_at), (shards_of,), jnp.float32, low / len(split), high / len(split))
        return jnp.repeat(jnp.exp(steps), shape[axis_at] // shards_of).reshape((-1,) + (1,) * (len(shape) - axis_at - 1))

    factor_of = one(*split[0])
    for cut in split[1:]:
        factor_of = factor_of * one(*cut)
    return factor_of


def bell_draw(stream_key, extent, scale, limit, shards=(), kind=jnp.bfloat16):
    values = scale * jax.random.normal(stream_key, extent, jnp.float32)
    if shards:
        values = values * shard_levels(stream_key, extent, shards, -0.22, 0.18)
    return jnp.clip(values, -limit, limit).astype(kind)


def setup_inputs(seed: int = 0) -> dict:
    splits = jax.random.split(jax.random.key(seed), 9)
    return {
        "samples_w": bell_draw(splits[0], (CELLS, SAMPLES), 1.0, 6.0, ((0, 64), (1, 4))),
        "dense_tiles": bell_draw(splits[1], (CELLS, B), B ** -0.5, 0.1875, ((0, 256),)),
        "left_factors": bell_draw(splits[2], (CELLS, TILES * R), (TILES * R) ** -0.5, 0.125, ((0, 64),)),
        "right_factors": bell_draw(splits[3], (CELLS, TILES * R), B ** -0.5, 0.1875, ((0, 64),)),
        "ranks": plant(jax.random.randint(splits[4], (TILES, TILES), R // 4, R + 1), jax.random.fold_in(splits[4], 1), R // 4, R).astype(jnp.int32),
        "area_blocks": bell_draw(splits[5], (TILES * AREAS, B), (B * TILES // GROUPS) ** -0.5, 0.03125, ((0, 64),)),
        "area_group": plant(jax.random.randint(splits[6], (TILES,), 0, GROUPS), jax.random.fold_in(splits[6], 1), 0, GROUPS - 1).astype(jnp.int32),
        "counts": plant(jax.random.randint(splits[7], (GROUPS * AREAS,), 0, 6), jax.random.fold_in(splits[7], 1), 0, 5).astype(jnp.int32),
    }


def rank_mask(ranks):
    rank_steps = jnp.arange(R, dtype=jnp.int32)
    return (rank_steps[None, None, :] < ranks[:, :, None]).astype(jnp.float32)


def area_gradient(linear, counts):
    rate = 1.0 + jax.nn.softplus(linear)
    return (jax.nn.sigmoid(linear) * (counts.astype(jnp.float32)[:, None] / rate - 1.0)).astype(jnp.bfloat16)


def reference(samples_w, dense_tiles, left_factors, right_factors, ranks, area_blocks, area_group, counts):
    tile_count = CELLS // B
    sample_count = samples_w.shape[1]
    mask_all = rank_mask(ranks)
    w_tiles = samples_w.reshape(tile_count, B, sample_count)
    right_tiles = right_factors.reshape(tile_count, B, tile_count * R)
    left_tiles = left_factors.reshape(tile_count, B, tile_count * R)
    dense_blocks = dense_tiles.reshape(tile_count, B, B)

    def project(pair):
        factor, values = pair
        return jnp.dot(factor.T, values, preferred_element_type=jnp.float32)

    coeff = lax.map(project, (right_tiles, w_tiles))
    coeff = coeff.reshape(tile_count, tile_count, R, sample_count) * jnp.transpose(mask_all, (1, 0, 2))[:, :, :, None]
    coeff = coeff.astype(jnp.bfloat16)
    coeff = jnp.transpose(coeff, (1, 0, 2, 3)).reshape(tile_count, tile_count * R, sample_count)

    def forward_field(items):
        factor, coeff_row, dense_one, values = items
        low_rank = jnp.dot(factor, coeff_row, preferred_element_type=jnp.float32)
        return (low_rank + jnp.dot(dense_one, values, preferred_element_type=jnp.float32)).astype(jnp.bfloat16)

    field = lax.map(forward_field, (left_tiles, coeff, dense_blocks, w_tiles))
    blocks = area_blocks.reshape(tile_count, AREAS, B)
    group_hot = (area_group[:, None] == jnp.arange(GROUPS, dtype=jnp.int32)[None, :]).astype(jnp.float32)

    def add_tile(total, items):
        block, field_tile, hot_row = items
        partial_eta = jnp.dot(block, field_tile, preferred_element_type=jnp.float32)
        return total + hot_row[:, None, None] * partial_eta[None], None

    linear, _ = lax.scan(add_tile, jnp.zeros((GROUPS, AREAS, sample_count), jnp.float32), (blocks, field, group_hot))
    grad = area_gradient(linear.reshape(GROUPS * AREAS, sample_count), counts)
    grad_groups = grad.reshape(GROUPS, AREAS, sample_count)

    def backward_tile(items):
        block, group_id = items
        chosen = lax.dynamic_index_in_dim(grad_groups, group_id, 0, keepdims=False)
        return jnp.dot(block.T, chosen, preferred_element_type=jnp.float32).astype(jnp.bfloat16)

    back = lax.map(backward_tile, (blocks, area_group))
    back_coeff = lax.map(project, (left_tiles, back))
    back_coeff = (back_coeff.reshape(tile_count, tile_count, R, sample_count) * mask_all[:, :, :, None]).astype(jnp.bfloat16)
    back_coeff = jnp.transpose(back_coeff, (1, 0, 2, 3)).reshape(tile_count, tile_count * R, sample_count)

    def backward_field(items):
        factor, coeff_col, dense_one, back_one = items
        low_rank = jnp.dot(factor, coeff_col, preferred_element_type=jnp.float32)
        return (low_rank + jnp.dot(dense_one.T, back_one, preferred_element_type=jnp.float32)).astype(jnp.bfloat16)

    result = lax.map(backward_field, (right_tiles, back_coeff, dense_blocks, back))
    return grad, result.reshape(CELLS, sample_count)
```

```python
import jax
import jax.numpy as jnp
from jax import lax
from jax.sharding import Mesh, PartitionSpec as P

AREAS = 1024
GROUPS = 2
TILE = ("z", "x", "c")
PLANE = ("x", "c")
F32 = jnp.float32
BF16 = jnp.bfloat16


def ring(size, shift):
    return [(i, (i + shift) % size) for i in range(size)]


def gather_dense(block):
    y = lax.axis_index("y")
    half = block.shape[0] // 2
    before = lax.ppermute(block, "y", ring(4, 1))
    after = lax.ppermute(block, "y", ring(4, -1))
    far_top = lax.ppermute(before[:half], "y", ring(4, 1))
    far_low = lax.ppermute(after[half:], "y", ring(4, -1))
    far = jnp.concatenate([far_top, far_low], axis=0)
    stacked = jnp.stack([block, before, far, after])
    return jnp.concatenate([stacked[(y - k) % 4] for k in range(4)], axis=0)


def plane_groups(area_group, b):
    slots = jnp.where(jnp.arange(8, dtype=jnp.int32) == b, area_group[0], 0)
    slots = jnp.broadcast_to(slots[:, None], (8, 128))
    for shift in (4, 2, 1):
        slots = slots + lax.ppermute(slots, PLANE, ring(8, shift))
    return slots[:, 0]


def area_gradient(linear, counts):
    rate = 1.0 + jax.nn.softplus(linear)
    return (jax.nn.sigmoid(linear) * (counts.astype(F32)[..., None] / rate - 1.0)).astype(BF16)


def exchange(values, axes):
    return lax.all_to_all(values, axes, split_axis=0, concat_axis=0, tiled=True)


def local(
    samples_w, dense_tiles, left_factors, right_factors, ranks, area_blocks, area_group, counts
):
    z = lax.axis_index("z")
    b = lax.axis_index(PLANE)
    groups = plane_groups(area_group, b)
    rank_steps = jnp.arange(32, dtype=jnp.int32)
    rank_keep = rank_steps[None, :] < ranks
    coeff_out = jnp.dot(right_factors.T, samples_w, preferred_element_type=F32)
    coeff_out = jnp.where(rank_keep[:, :, None], coeff_out.reshape(64, 32, 256), 0.0).astype(BF16)
    arrived = exchange(coeff_out, TILE).reshape(2048, 256)
    low_rank = jnp.dot(left_factors, arrived, preferred_element_type=F32)
    dense_full = gather_dense(dense_tiles)
    near_part = jnp.dot(dense_full, samples_w, preferred_element_type=F32)
    field_tile = (low_rank + near_part).astype(BF16)
    partial_eta = jnp.dot(area_blocks, field_tile, preferred_element_type=F32).astype(BF16)
    parts = exchange(partial_eta.reshape(8, 128, 256), PLANE).astype(F32)
    in_group = (groups[None, :] == jnp.arange(GROUPS, dtype=jnp.int32)[:, None])
    both = jnp.stack(
        [jnp.sum(jnp.where(in_group[g][:, None, None], parts, 0.0), axis=0) for g in range(GROUPS)]
    ).astype(BF16)
    by_z = jnp.transpose(both.reshape(GROUPS, 8, 16, 256), (1, 0, 2, 3))
    linear = jnp.sum(exchange(by_z, ("z",)).astype(F32), axis=0)
    counts_here = lax.dynamic_index_in_dim(counts.reshape(GROUPS, 64, 16), b * 8 + z, 1, False)
    grad = area_gradient(linear, counts_here)
    grads_z = exchange(jnp.broadcast_to(grad[None], (8, GROUPS, 16, 256)), ("z",))
    block = jnp.transpose(grads_z, (1, 0, 2, 3)).reshape(GROUPS, 128, 256)
    wanted = jnp.where(groups[:, None, None] == 0, block[0][None], block[1][None])
    shown = jnp.where(z < 4, block[0], block[1]).reshape(4, 32, 256)
    shown = jnp.concatenate([shown, shown], axis=0)
    got = exchange(jnp.concatenate([wanted, shown], axis=1), PLANE)
    grad_group = got[:, :128].reshape(AREAS, 256)
    grad_out = lax.dynamic_index_in_dim(got[:, 128:], (z % 4) * 2 + b // 4, 0, False)
    back_tile = jnp.dot(area_blocks.T, grad_group, preferred_element_type=F32).astype(BF16)
    back_coeff = jnp.dot(left_factors.T, back_tile, preferred_element_type=F32).astype(BF16)
    returned = exchange(back_coeff.reshape(64, 32, 256), TILE)
    returned = jnp.where(rank_keep[:, :, None], returned, jnp.zeros((), BF16)).reshape(2048, 256)
    low_back = jnp.dot(right_factors, returned, preferred_element_type=F32)
    near_back = jnp.dot(dense_full.T, back_tile, preferred_element_type=F32)
    return grad_out, (low_back + near_back).astype(BF16)


def solution(mesh):
    plane = Mesh(mesh.devices.reshape(8, 4, 2, 4), ("z", "x", "c", "y"))
    return jax.shard_map(
        local,
        mesh=plane,
        in_specs=(
            P(TILE, "y"),
            P(("z", "x", "c", "y"), None),
            P(TILE, None),
            P(TILE, None),
            P(None, TILE),
            P(TILE, None),
            P(TILE),
            P(),
        ),
        out_specs=(P(TILE, "y"), P(TILE, "y")),
        check_vma=False,
    )
```

```python
import jax
import jax.numpy as jnp
from jax import lax
from jax.sharding import Mesh, PartitionSpec as P

GROUPS = 2
TILE = ("z", "x", "c")
PLANE = ("x", "c")
F32 = jnp.float32
BF16 = jnp.bfloat16


def ring(size, shift):
    return [(i, (i + shift) % size) for i in range(size)]


def gather_y(block):
    half = block.shape[0] // 2
    before = lax.ppermute(block, "y", ring(4, 1))
    after = lax.ppermute(block, "y", ring(4, -1))
    far_top = lax.ppermute(before[:half], "y", ring(4, 1))
    far_low = lax.ppermute(after[half:], "y", ring(4, -1))
    return block, before, (far_top, far_low), after


def tile_groups(area_group, z, b):
    here = (lax.broadcasted_iota(jnp.int32, (8, 128), 0) == z) & (
        lax.broadcasted_iota(jnp.int32, (8, 128), 1) == b
    )
    slots = jnp.where(here, area_group[0], 0)
    for shift in (4, 2, 1):
        slots = slots + lax.ppermute(slots, PLANE, ring(8, shift))
    for shift in (4, 2, 1):
        slots = slots + lax.ppermute(slots, "z", ring(8, shift))
    return slots[:, :8].reshape(64)


def area_gradient(linear, counts):
    rate = 1.0 + jax.nn.softplus(linear)
    return (jax.nn.sigmoid(linear) * (counts.astype(F32)[..., None] / rate - 1.0)).astype(BF16)


def exchange(values, axes):
    return lax.all_to_all(values, axes, split_axis=0, concat_axis=0, tiled=True)


def dot(a, b, ca, cb):
    return lax.dot_general(a, b, (((ca,), (cb,)), ((), ())), preferred_element_type=F32)


def at(values, index, axis=0):
    return lax.dynamic_index_in_dim(values, index, axis, keepdims=False)


def local(
    samples_w, dense_tiles, left_factors, right_factors, ranks, area_blocks, area_group, counts
):
    z, x, c, y = (lax.axis_index(a) for a in ("z", "x", "c", "y"))
    k = (z * 4 + x) * 2 + c
    rows_y = at(area_blocks.reshape(32, 4, 8, 1024), y, 1)
    rows_y = jnp.transpose(rows_y.reshape(4, 4, 2, 8, 1024), (2, 1, 0, 3, 4)).reshape(256, 1024)
    sent = dot(left_factors, rows_y, 0, 1).astype(BF16)
    came = exchange(sent.reshape(64, 32, 256), TILE)

    groups = tile_groups(area_group, z, x * 2 + c)
    w_own, w_before, w_far, w_after = gather_y(samples_w)
    w_all = jnp.concatenate([w_own, w_before, jnp.concatenate(w_far, axis=0), w_after], axis=1)
    d_own, d_before, d_far, d_after = gather_y(dense_tiles)

    def near(block, s, first=0):
        cols = lax.dynamic_slice_in_dim(
            rows_y, (y - s) % 4 * 256 + first, block.shape[0], axis=1
        )
        return dot(cols, block, 1, 0)

    near_part = (
        near(d_own, 0) + near(d_before, 1) + near(d_far[0], 2) + near(d_far[1], 2, 128)
        + near(d_after, 3)
    )

    rank_keep = jnp.arange(32, dtype=jnp.int32)[None, :] < ranks
    both = jnp.concatenate(
        [
            jnp.where((rank_keep & (groups == g)[:, None])[:, :, None], came, jnp.zeros((), BF16))
            for g in range(GROUPS)
        ],
        axis=2,
    ).reshape(2048, 512)
    operator = dot(both, right_factors, 0, 1).reshape(GROUPS, 256, 1024)
    hot = (area_group[0] == jnp.arange(GROUPS, dtype=jnp.int32)).astype(F32)
    operator = (operator + hot[:, None, None] * near_part[None]).astype(BF16)
    operator = operator.reshape(GROUPS, 8, 32, 1024)
    operator = jnp.stack(
        [at(operator, (c + dc) % 2 * 4 + (x - dx) % 4, 1) for dc in range(2) for dx in range(4)]
    ).reshape(512, 1024)
    partial_eta = dot(operator, w_all, 1, 0).astype(BF16)
    m_own, m_before, m_far, m_after = gather_y(operator)

    halves = partial_eta.reshape(2, 4, 64, 1024)
    core_sum = halves[0].astype(F32) + lax.ppermute(halves[1], "c", ring(2, 1)).astype(F32)
    core_sum = core_sum.astype(BF16)
    x_sum = core_sum[0].astype(F32)
    for s in (2, 1, 3):
        x_sum = x_sum + lax.ppermute(core_sum[s], "x", ring(4, -s)).astype(F32)
    z_parts = exchange(x_sum.astype(BF16).reshape(8, 8, 1024), ("z",))
    linear = jnp.sum(z_parts.astype(F32), axis=0)
    grad = area_gradient(linear, counts.reshape(64, 4, 8)[k, y])

    pieces = grad.reshape(8, 4, 256)
    by_y = jnp.stack([at(pieces, (y - t) % 4, 1) for t in range(4)])
    got = exchange(jnp.broadcast_to(by_y[None], (8, 4, 8, 256)).reshape(32, 8, 256), ("z", "y"))
    got = got.reshape(8, 4, 8, 256)
    grad_out = at(got, z).reshape(32, 256)
    g_own = jnp.stack([at(got, (y - s) % 4, 1) for s in range(4)])
    by_x = [g_own] + [lax.ppermute(g_own, "x", ring(4, s)) for s in (1, 2, 3)]
    row = jnp.stack(by_x, axis=1).reshape(4, 4, 64, 256)
    other = lax.ppermute(row, "c", ring(2, 1))
    grad_all = jnp.stack([row, other], axis=1).reshape(2048, 256)
    m_all = jnp.concatenate([m_own, m_before, *m_far, m_after], axis=0)
    return grad_out, dot(m_all, grad_all, 0, 0).astype(BF16)


def solution(mesh):
    plane = Mesh(mesh.devices.reshape(8, 4, 2, 4), ("z", "x", "c", "y"))
    return jax.shard_map(
        local,
        mesh=plane,
        in_specs=(
            P(TILE, "y"),
            P(("z", "x", "c", "y"), None),
            P(TILE, None),
            P(TILE, None),
            P(None, TILE),
            P(TILE, None),
            P(TILE),
            P(),
        ),
        out_specs=(P(TILE, "y"), P(TILE, "y")),
        check_vma=False,
    )
```

```python
import functools

import jax
import jax.numpy as jnp
from jax import lax
from jax.experimental import pallas as pl
from jax.experimental.pallas import tpu as pltpu
from jax.sharding import Mesh, PartitionSpec as P

GROUPS = 2
TILE = ("z", "x", "c")
F32 = jnp.float32
BF16 = jnp.bfloat16


def ring(size, shift):
    return [(i, (i + shift) % size) for i in range(size)]


def dot(a, b, ca, cb):
    return lax.dot_general(a, b, (((ca,), (cb,)), ((), ())), preferred_element_type=F32)


def at(values, index, axis=0):
    return lax.dynamic_index_in_dim(values, index, axis, keepdims=False)


def gather_y(block):
    half = block.shape[0] // 2
    before = lax.ppermute(block, "y", ring(4, 1))
    after = lax.ppermute(block, "y", ring(4, -1))
    far_top = lax.ppermute(before[:half], "y", ring(4, 1))
    far_low = lax.ppermute(after[half:], "y", ring(4, -1))
    return block, before, (far_top, far_low), after


def area_gradient(linear, counts):
    rate = 1.0 + jax.nn.softplus(linear)
    return (jax.nn.sigmoid(linear) * (counts.astype(F32)[..., None] / rate - 1.0)).astype(BF16)


def exchange(values, axes):
    return lax.all_to_all(values, axes, split_axis=0, concat_axis=0, tiled=True)


def messages_kernel(place, rows_ref, left_ref, out_ref, rows_sc):
    @pl.when(pl.program_id(0) == 0)
    def _():
        rows_sc[...] = rows_ref[...].reshape(256, 1024)

    part = dot(rows_sc[...], left_ref[...], 1, 0)
    part = part.T.astype(BF16).reshape(8, 32, 256)
    out_ref[:, 0:32, :] = part[:, :, :128]
    out_ref[:, 32:64, :] = part[:, :, 128:]
    out_ref[:, 64:72, :] = jnp.full((8, 8, 128), place[1], jnp.int32).astype(F32).astype(BF16)


def messages(place, area_blocks, left_factors):
    return pl.pallas_call(
        messages_kernel,
        grid_spec=pltpu.PrefetchScalarGridSpec(
            num_scalar_prefetch=1,
            grid=(8,),
            in_specs=[
                pl.BlockSpec((32, None, 8, 1024), lambda i, p: (0, p[0], 0, 0)),
                pl.BlockSpec((1024, 256), lambda i, p: (0, i)),
            ],
            out_specs=pl.BlockSpec((8, 72, 128), lambda i, p: (i, 0, 0)),
            scratch_shapes=[pltpu.VMEM((256, 1024), BF16)],
        ),
        out_shape=jax.ShapeDtypeStruct((64, 72, 128), BF16),
        compiler_params=pltpu.CompilerParams(vmem_limit_bytes=24 << 20),
        cost_estimate=pl.CostEstimate(
            flops=2 * 256 * 1024 * 2048, bytes_accessed=6 << 20, transcendentals=0
        ),
        name="messages",
    )(place, area_blocks.reshape(32, 4, 8, 1024), left_factors)


def operator_kernel(
    place, came_hbm, right_hbm, near_hbm, w_hbm, keep_ref, op_ref, eta_ref,
    came, right, near, w, lhs, op, sems,
):
    copies = [
        pltpu.make_async_copy(came_hbm, came, sems.at[0]),
        pltpu.make_async_copy(right_hbm, right, sems.at[1]),
        pltpu.make_async_copy(near_hbm, near, sems.at[2]),
        pltpu.make_async_copy(w_hbm, w, sems.at[3]),
    ]
    for copy in copies:
        copy.start()
    x, c, group = place[0], place[1], place[2]
    eye = (
        lax.broadcasted_iota(jnp.int32, (128, 128), 0)
        == lax.broadcasted_iota(jnp.int32, (128, 128), 1)
    ).astype(F32).astype(BF16)
    copies[0].wait()

    @pl.loop(0, 4)
    def _(n):
        first = pl.multiple_of(n * 512, 512)
        lanes = pl.ds(first, 512)
        tiles = pl.ds(n * 16, 16)
        ids = came[tiles, 64:72, :]
        ids = jnp.concatenate([ids] * 4, axis=1).reshape(512, 128)
        ids = dot(eye[:8], ids, 1, 1)[0:1]
        keep = keep_ref[:, lanes]
        for h in range(2):
            part = dot(eye, came[tiles, 32 * h : 32 * h + 32, :].reshape(512, 128), 1, 1)
            for g in range(GROUPS):
                mask = keep * (ids == g).astype(F32)
                lhs[g * 256 + h * 128 : g * 256 + h * 128 + 128, lanes] = (
                    jnp.where(mask > 0.5, part, 0.0).astype(BF16)
                )

    copies[1].wait()
    copies[2].wait()
    hot = [jnp.where(group == g, 1.0, 0.0) for g in range(GROUPS)]

    @pl.loop(0, 4)
    def _(n):
        first = pl.multiple_of(n * 256, 256)
        cells = pl.ds(first, 256)
        block = dot(lhs[...], right[cells, :], 1, 1)
        extra = near[:, cells]
        for g in range(GROUPS):
            rows = slice(g * 256, g * 256 + 256)
            op[rows, cells] = block[rows] + hot[g] * extra

    for dc in range(2):
        for dx in range(4):
            owner = lax.rem(x - dx + 4, 4) * 2 + lax.rem(c + dc, 2)
            pieces = [
                op[pl.ds(pl.multiple_of((low * 8 + owner) * 8 + g * 256, 8), 8), :]
                for g in range(GROUPS)
                for low in range(4)
            ]
            first = (dc * 4 + dx) * 64
            op_ref[first : first + 64, :] = jnp.concatenate(pieces, axis=0).astype(BF16)
    copies[3].wait()

    @pl.loop(0, 4)
    def _(n):
        first = pl.multiple_of(n * 256, 256)
        cols = pl.ds(first, 256)
        eta_ref[:, cols] = dot(op_ref[...], w[:, cols], 1, 0).astype(BF16)


def operator(place, came, right_factors, near_part, w_all, keep):
    return pl.pallas_call(
        operator_kernel,
        grid_spec=pltpu.PrefetchScalarGridSpec(
            num_scalar_prefetch=1,
            grid=(),
            in_specs=[pl.BlockSpec(memory_space=pl.ANY)] * 4
            + [pl.BlockSpec(memory_space=pltpu.VMEM)],
            out_specs=[pl.BlockSpec(memory_space=pltpu.VMEM)] * 2,
            scratch_shapes=[
                pltpu.VMEM((64, 72, 128), BF16),
                pltpu.VMEM((1024, 2048), BF16),
                pltpu.VMEM((256, 1024), F32),
                pltpu.VMEM((1024, 1024), BF16),
                pltpu.VMEM((512, 2048), BF16),
                pltpu.VMEM((512, 1024), F32),
                pltpu.SemaphoreType.DMA((4,)),
            ],
        ),
        out_shape=[jax.ShapeDtypeStruct((512, 1024), BF16)] * 2,
        compiler_params=pltpu.CompilerParams(vmem_limit_bytes=32 << 20),
        cost_estimate=pl.CostEstimate(
            flops=2 * 512 * 1024 * 3072, bytes_accessed=11 << 20, transcendentals=0
        ),
        name="operator",
    )(place, came, right_factors, near_part, w_all, keep)


def local(
    samples_w, dense_tiles, left_factors, right_factors, ranks, area_blocks, area_group, counts
):
    z, x, c, y = (lax.axis_index(a) for a in ("z", "x", "c", "y"))
    k = (z * 4 + x) * 2 + c
    group = area_group[0]
    sent = messages(jnp.stack([y, group]), area_blocks, left_factors)
    came = exchange(sent, TILE)

    w_own, w_before, w_far, w_after = gather_y(samples_w)
    w_all = jnp.concatenate([w_own, w_before, jnp.concatenate(w_far, axis=0), w_after], axis=1)
    d_own, d_before, d_far, d_after = gather_y(dense_tiles)
    rows_y = at(area_blocks.reshape(32, 4, 8, 1024), y, 1).reshape(256, 1024)

    def near(block, s, first=0):
        cols = lax.dynamic_slice_in_dim(
            rows_y, (y - s) % 4 * 256 + first, block.shape[0], axis=1
        )
        return dot(cols, block, 1, 0)

    near_part = (
        near(d_own, 0) + near(d_before, 1) + near(d_far[0], 2) + near(d_far[1], 2, 128)
        + near(d_after, 3)
    )
    keep = (jnp.arange(32, dtype=jnp.int32)[None, :] < ranks).astype(F32).reshape(1, 2048)
    m_own, partial_eta = operator(
        jnp.stack([x, c, group]), came, right_factors, near_part, w_all, keep
    )
    m_own, m_before, m_far, m_after = gather_y(m_own)

    halves = partial_eta.reshape(2, 4, 64, 1024)
    core_sum = halves[0].astype(F32) + lax.ppermute(halves[1], "c", ring(2, 1)).astype(F32)
    core_sum = core_sum.astype(BF16)
    x_sum = core_sum[0].astype(F32)
    for s in (2, 1, 3):
        x_sum = x_sum + lax.ppermute(core_sum[s], "x", ring(4, -s)).astype(F32)
    z_parts = exchange(x_sum.astype(BF16).reshape(8, 8, 1024), ("z",))
    linear = jnp.sum(z_parts.astype(F32), axis=0)
    grad = area_gradient(linear, counts.reshape(64, 4, 8)[k, y])

    pieces = grad.reshape(8, 4, 256)
    by_y = jnp.stack([at(pieces, (y - t) % 4, 1) for t in range(4)])
    got = exchange(jnp.broadcast_to(by_y[None], (8, 4, 8, 256)).reshape(32, 8, 256), ("z", "y"))
    got = got.reshape(8, 4, 8, 256)
    grad_out = at(got, z).reshape(32, 256)
    g_own = jnp.stack([at(got, (y - s) % 4, 1) for s in range(4)])
    by_x = [g_own] + [lax.ppermute(g_own, "x", ring(4, s)) for s in (1, 2, 3)]
    row = jnp.stack(by_x, axis=1).reshape(4, 4, 64, 256)
    other = lax.ppermute(row, "c", ring(2, 1))
    grad_all = jnp.stack([row, other], axis=1).reshape(2048, 256)
    m_all = jnp.concatenate([m_own, m_before, *m_far, m_after], axis=0)
    return grad_out, dot(m_all, grad_all, 0, 0).astype(BF16)


def solution(mesh):
    plane = Mesh(mesh.devices.reshape(8, 4, 2, 4), ("z", "x", "c", "y"))
    return jax.shard_map(
        local,
        mesh=plane,
        in_specs=(
            P(TILE, "y"),
            P(("z", "x", "c", "y"), None),
            P(TILE, None),
            P(TILE, None),
            P(None, TILE),
            P(TILE, None),
            P(TILE),
            P(),
        ),
        out_specs=(P(TILE, "y"), P(TILE, "y")),
        check_vma=False,
    )
```

```python
import jax
import jax.numpy as jnp
from jax import lax
from jax.experimental import pallas as pl
from jax.experimental.pallas import tpu as pltpu
from jax.sharding import Mesh, PartitionSpec as P


GROUPS = 2
TILE = ("z", "x", "c")
F32 = jnp.float32
BF16 = jnp.bfloat16
VMEM_GRANT = 60 << 20


def ring(size, shift):
    return [(i, (i + shift) % size) for i in range(size)]


def dot(a, b, ca, cb):
    return lax.dot_general(a, b, (((ca,), (cb,)), ((), ())), preferred_element_type=F32)


def at(values, index, axis=0):
    return lax.dynamic_index_in_dim(values, index, axis, keepdims=False)


def area_gradient(linear, counts):
    rate = 1.0 + jax.nn.softplus(linear)
    return (jax.nn.sigmoid(linear) * (counts.astype(F32)[..., None] / rate - 1.0)).astype(BF16)


def exchange(values, axes):
    return lax.all_to_all(values, axes, split_axis=0, concat_axis=0, tiled=True)


def identity(size):
    return (
        lax.broadcasted_iota(jnp.int32, (size, size), 0)
        == lax.broadcasted_iota(jnp.int32, (size, size), 1)
    ).astype(F32).astype(BF16)


def messages_kernel(place, rows_ref, left_ref, out_ref, rows_out, rows_sc):
    @pl.when(pl.program_id(0) == 0)
    def _():
        rows = rows_ref[...].reshape(256, 1024)
        rows_sc[...] = rows
        rows_out[...] = rows

    part = dot(rows_sc[...], left_ref[...], 1, 0).astype(BF16)
    eye = identity(256)
    for half in range(2):
        block = dot(eye, part[:, half * 256 : half * 256 + 256], 1, 1).astype(BF16)
        block = block.reshape(8, 32, 256)
        out_ref[half * 8 : half * 8 + 8, 0:32, :] = block[:, :, :128]
        out_ref[half * 8 : half * 8 + 8, 32:64, :] = block[:, :, 128:]
    out_ref[:, 64:72, :] = jnp.full((16, 8, 128), place[1], jnp.int32).astype(F32).astype(BF16)


def messages(place, area_blocks, left_factors):
    return pl.pallas_call(
        messages_kernel,
        grid_spec=pltpu.PrefetchScalarGridSpec(
            num_scalar_prefetch=1,
            grid=(4,),
            in_specs=[
                pl.BlockSpec((32, None, 8, 1024), lambda i, p: (0, p[0], 0, 0)),
                pl.BlockSpec((1024, 512), lambda i, p: (0, i)),
            ],
            out_specs=[
                pl.BlockSpec((16, 72, 128), lambda i, p: (i, 0, 0)),
                pl.BlockSpec((256, 1024), lambda i, p: (0, 0)),
            ],
            scratch_shapes=[pltpu.VMEM((256, 1024), BF16)],
        ),
        out_shape=[
            jax.ShapeDtypeStruct((64, 72, 128), BF16),
            jax.ShapeDtypeStruct((256, 1024), BF16),
        ],
        compiler_params=pltpu.CompilerParams(vmem_limit_bytes=VMEM_GRANT),
        cost_estimate=pl.CostEstimate(
            flops=2 * 256 * 1024 * 2048, bytes_accessed=6 << 20, transcendentals=0
        ),
        name="messages",
    )(place, area_blocks.reshape(32, 4, 8, 1024), left_factors)


def operator_kernel(place, *refs):
    keep_ref, sources = refs[0], refs[1:14]
    op_refs, eta_refs = refs[14:16], refs[16:18]
    held, lhs, op, sems = refs[18:31], refs[31], refs[32], refs[33]
    copies = [
        pltpu.make_async_copy(source, target, sems.at[n])
        for n, (source, target) in enumerate(zip(sources, held))
    ]
    for copy in copies:
        copy.start()
    came, right, rows = held[:3]
    near, w = held[3:8], held[8:13]
    x, c, y, group = place[0], place[1], place[2], place[3]
    eye = identity(128)
    copies[0].wait()

    @pl.loop(0, 4)
    def _(n):
        lanes = pl.ds(pl.multiple_of(n * 512, 512), 512)
        tiles = pl.ds(n * 16, 16)
        ids = came[tiles, 64:72, :]
        ids = jnp.concatenate([ids] * 4, axis=1).reshape(512, 128)
        ids = dot(eye[:8], ids, 1, 1)[0:1]
        keep = keep_ref[:, lanes]
        for h in range(2):
            part = dot(eye, came[tiles, 32 * h : 32 * h + 32, :].reshape(512, 128), 1, 1)
            for g in range(GROUPS):
                mask = keep * (ids == g).astype(F32)
                lhs[g * 256 + h * 128 : g * 256 + h * 128 + 128, lanes] = (
                    jnp.where(mask > 0.5, part, 0.0).astype(BF16)
                )

    for copy in copies[1:8]:
        copy.wait()
    hot = [jnp.where(group == g, 1.0, 0.0) for g in range(GROUPS)]
    starts = [
        pl.multiple_of(lax.rem(y - s + 4, 4) * 256 + f, 128)
        for s, f in ((0, 0), (1, 0), (2, 0), (2, 128), (3, 0))
    ]

    @pl.loop(0, 4)
    def _(n):
        cells = pl.ds(pl.multiple_of(n * 256, 256), 256)
        extra = jnp.zeros((256, 256), F32)
        for piece, first in zip(near, starts):
            extra += dot(rows[:, pl.ds(first, piece.shape[0])], piece[:, cells], 1, 0)
        block = dot(lhs[...], right[cells, :], 1, 1)
        for g in range(GROUPS):
            span = slice(g * 256, g * 256 + 256)
            op[span, cells] = block[span] + hot[g] * extra

    for dc in range(2):
        for dx in range(4):
            owner = lax.rem(x - dx + 4, 4) * 2 + lax.rem(c + dc, 2)
            pieces = [
                op[pl.ds(pl.multiple_of((low * 8 + owner) * 8 + g * 256, 8), 8), :]
                for g in range(GROUPS)
                for low in range(4)
            ]
            op_refs[dc][dx * 64 : dx * 64 + 64, :] = jnp.concatenate(pieces, axis=0).astype(BF16)
    for copy in copies[8:]:
        copy.wait()
    for dc in range(2):
        for s, piece in ((0, w[0]), (1, w[1]), (3, w[4])):
            eta_refs[dc][:, s * 256 : s * 256 + 256] = dot(
                op_refs[dc][...], piece[...], 1, 0
            ).astype(BF16)
        eta_refs[dc][:, 512:768] = (
            dot(op_refs[dc][:, :512], w[2][...], 1, 0) + dot(op_refs[dc][:, 512:], w[3][...], 1, 0)
        ).astype(BF16)


def operator(place, came, right_factors, rows, near, w, keep):
    sources = (came, right_factors, rows, *near, *w)
    return pl.pallas_call(
        operator_kernel,
        grid_spec=pltpu.PrefetchScalarGridSpec(
            num_scalar_prefetch=1,
            grid=(),
            in_specs=[pl.BlockSpec(memory_space=pltpu.VMEM)]
            + [pl.BlockSpec(memory_space=pl.ANY)] * len(sources),
            out_specs=[pl.BlockSpec(memory_space=pltpu.VMEM)] * 4,
            scratch_shapes=[pltpu.VMEM(v.shape, v.dtype) for v in sources]
            + [
                pltpu.VMEM((512, 2048), BF16),
                pltpu.VMEM((512, 1024), F32),
                pltpu.SemaphoreType.DMA((len(sources),)),
            ],
        ),
        out_shape=[jax.ShapeDtypeStruct((256, 1024), BF16)] * 4,
        compiler_params=pltpu.CompilerParams(vmem_limit_bytes=VMEM_GRANT),
        cost_estimate=pl.CostEstimate(
            flops=2 * 512 * 1024 * 3072, bytes_accessed=11 << 20, transcendentals=0
        ),
        name="operator",
    )(place, keep, *sources)


def gather_y(block):
    half = block.shape[0] // 2
    before = lax.ppermute(block, "y", ring(4, 1))
    after = lax.ppermute(block, "y", ring(4, -1))
    far_top = lax.ppermute(before[:half], "y", ring(4, 1))
    far_low = lax.ppermute(after[half:], "y", ring(4, -1))
    return block, before, far_top, far_low, after


def step(
    samples_w, dense_tiles, left_factors, right_factors, ranks, area_blocks, area_group, counts
):
    z, x, c, y = (lax.axis_index(a) for a in ("z", "x", "c", "y"))
    k = (z * 4 + x) * 2 + c
    group = area_group[0]
    w = gather_y(samples_w)
    sent, rows = messages(jnp.stack([y, group]), area_blocks, left_factors)
    came = exchange(sent, TILE)
    near = gather_y(dense_tiles)
    keep = (jnp.arange(32, dtype=jnp.int32)[None, :] < ranks).astype(F32).reshape(1, 2048)
    top, low, eta_keep, eta_send = operator(
        jnp.stack([x, c, y, group]), came, right_factors, rows, near, w, keep
    )
    eta_came = lax.ppermute(eta_send, "c", ring(2, 1))
    top_before = lax.ppermute(top, "y", ring(4, 1))
    low_after = lax.ppermute(low, "y", ring(4, -1))
    low_before = lax.ppermute(low, "y", ring(4, 1))
    top_after = lax.ppermute(top, "y", ring(4, -1))
    top_far = lax.ppermute(top_before, "y", ring(4, 1))
    low_far = lax.ppermute(low_after, "y", ring(4, -1))
    core_sum = (eta_keep.astype(F32) + eta_came.astype(F32)).astype(BF16).reshape(4, 64, 1024)
    x_sum = core_sum[0].astype(F32)
    came_x = [lax.ppermute(core_sum[s], "x", ring(4, -s)) for s in (2, 1, 3)]
    for part in came_x:
        x_sum = x_sum + part.astype(F32)
    z_parts = exchange(x_sum.astype(BF16).reshape(8, 8, 1024), ("z",))
    linear = jnp.sum(z_parts.astype(F32), axis=0)
    grad = area_gradient(linear, counts.reshape(64, 4, 8)[k, y])

    pieces = grad.reshape(8, 4, 256)
    by_y = jnp.stack([at(pieces, (y - t) % 4, 1) for t in range(4)])
    got = exchange(
        jnp.broadcast_to(by_y[None], (8, 4, 8, 256)).reshape(32, 8, 256), ("z", "y")
    )
    got = got.reshape(8, 4, 8, 256)
    grad_out = at(got, z).reshape(32, 256)
    g_own = jnp.stack([at(got, (y - s) % 4, 1) for s in range(4)])
    by_x = {s: lax.ppermute(g_own, "x", ring(4, s)) for s in (2, 1, 3)}
    row = jnp.stack([g_own, by_x[1], by_x[2], by_x[3]], axis=1).reshape(1024, 256)
    other = lax.ppermute(row, "c", ring(2, 1))
    top_all = jnp.concatenate([top, top_before, top_far, top_after], axis=0)
    low_all = jnp.concatenate([low, low_before, low_far, low_after], axis=0)
    own_part = lax.optimization_barrier(dot(top_all, row, 0, 0))
    return grad_out, (own_part + dot(low_all, other, 0, 0)).astype(BF16)


def solution(mesh):
    plane = Mesh(mesh.devices.reshape(8, 4, 2, 4), ("z", "x", "c", "y"))
    return jax.shard_map(
        step,
        mesh=plane,
        in_specs=(
            P(TILE, "y"),
            P(("z", "x", "c", "y"), None),
            P(TILE, None),
            P(TILE, None),
            P(None, TILE),
            P(TILE, None),
            P(TILE),
            P(),
        ),
        out_specs=(P(TILE, "y"), P(TILE, "y")),
        check_vma=False,
    )
```

```python
import jax
import jax.numpy as jnp
from jax import lax
from jax.experimental import pallas as pl
from jax.experimental.pallas import tpu as pltpu
from jax.sharding import Mesh, PartitionSpec as P


GROUPS = 2
TILE = ("z", "x", "c")
F32 = jnp.float32
BF16 = jnp.bfloat16
VMEM_GRANT = 60 << 20


def ring(size, shift):
    return [(i, (i + shift) % size) for i in range(size)]


def dot(a, b, ca, cb):
    return lax.dot_general(a, b, (((ca,), (cb,)), ((), ())), preferred_element_type=F32)


def at(values, index, axis=0):
    return lax.dynamic_index_in_dim(values, index, axis, keepdims=False)


def area_gradient(linear, counts):
    rate = 1.0 + jax.nn.softplus(linear)
    return (jax.nn.sigmoid(linear) * (counts.astype(F32)[..., None] / rate - 1.0)).astype(BF16)


def exchange(values, axes):
    return lax.all_to_all(values, axes, split_axis=0, concat_axis=0, tiled=True)


def identity(size):
    return (
        lax.broadcasted_iota(jnp.int32, (size, size), 0)
        == lax.broadcasted_iota(jnp.int32, (size, size), 1)
    ).astype(F32).astype(BF16)


def messages_kernel(place, rows_hbm, left_hbm, out_hbm, rows_out, parts, left, out, sems):
    y = lax.axis_index("y")
    first = pltpu.make_async_copy(rows_hbm.at[:, y], parts, sems.at[0])
    first.start()
    loads = []
    for n in range(4):
        cols = pl.ds(n * 512, 512)
        loads.append(pltpu.make_async_copy(left_hbm.at[:, cols], left.at[n], sems.at[1 + n]))
        loads[n].start()
    first.wait()
    rows_out[...] = parts[...].reshape(256, 1024)
    ids = jnp.full((16, 8, 128), place[0], jnp.int32).astype(F32).astype(BF16)
    eye = identity(256)
    stores = []
    for n in range(4):
        loads[n].wait()
        part = dot(rows_out[...], left[n], 1, 0).astype(BF16)
        for half in range(2):
            block = dot(eye, part[:, half * 256 : half * 256 + 256], 1, 1).astype(BF16)
            block = block.reshape(8, 32, 256)
            tiles = slice(n * 16 + half * 8, n * 16 + half * 8 + 8)
            out[tiles, 0:32, :] = block[:, :, :128]
            out[tiles, 32:64, :] = block[:, :, 128:]
        out[n * 16 : n * 16 + 16, 64:72, :] = ids
        tiles = pl.ds(n * 16, 16)
        stores.append(pltpu.make_async_copy(out.at[tiles], out_hbm.at[tiles], sems.at[5 + n]))
        stores[n].start()
    for store in stores:
        store.wait()


def messages(place, area_blocks, left_factors):
    return pl.pallas_call(
        messages_kernel,
        grid_spec=pltpu.PrefetchScalarGridSpec(
            num_scalar_prefetch=1,
            grid=(),
            in_specs=[pl.BlockSpec(memory_space=pltpu.HBM)] * 2,
            out_specs=[
                pl.BlockSpec(memory_space=pltpu.HBM),
                pl.BlockSpec(memory_space=pltpu.VMEM),
            ],
            scratch_shapes=[
                pltpu.VMEM((32, 8, 1024), BF16),
                pltpu.VMEM((4, 1024, 512), BF16),
                pltpu.VMEM((64, 72, 128), BF16),
                pltpu.SemaphoreType.DMA((9,)),
            ],
        ),
        out_shape=[
            jax.ShapeDtypeStruct((64, 72, 128), BF16),
            jax.ShapeDtypeStruct((256, 1024), BF16),
        ],
        compiler_params=pltpu.CompilerParams(vmem_limit_bytes=VMEM_GRANT),
        cost_estimate=pl.CostEstimate(
            flops=2 * 256 * 1024 * 2048, bytes_accessed=6 << 20, transcendentals=0
        ),
        name="messages",
    )(place, area_blocks.reshape(32, 4, 8, 1024), left_factors)


def in_vmem(kernel, outs, scratch, flops, grant):
    def call(place, *values):
        size = sum(v.size * v.dtype.itemsize for v in values)
        return pl.pallas_call(
            kernel,
            grid_spec=pltpu.PrefetchScalarGridSpec(
                num_scalar_prefetch=1,
                grid=(),
                in_specs=[pl.BlockSpec(memory_space=pltpu.VMEM)] * len(values),
                out_specs=[pl.BlockSpec(memory_space=pltpu.VMEM)] * len(outs),
                scratch_shapes=scratch,
            ),
            out_shape=[jax.ShapeDtypeStruct(*out) for out in outs],
            compiler_params=pltpu.CompilerParams(vmem_limit_bytes=grant << 20),
            cost_estimate=pl.CostEstimate(flops=flops, bytes_accessed=size, transcendentals=0),
        )(place, *values)

    return call


def offsets_matrix(x, c):
    row = lax.broadcasted_iota(jnp.int32, (256, 256), 0)
    dc, dx, low, r = row >> 7, (row >> 5) & 3, (row >> 3) & 3, row & 7
    area = low * 64 + ((x - dx) & 3) * 16 + ((c + dc) & 1) * 8 + r
    return (lax.broadcasted_iota(jnp.int32, (256, 256), 1) == area).astype(F32).astype(BF16)


def near_kernel(group, rows, *refs):
    d, near, turned = refs[:5], refs[5], refs[6]
    x, c, y = (lax.axis_index(a) for a in ("x", "c", "y"))
    turned[...] = dot(offsets_matrix(x, c), rows[...], 1, 0).astype(BF16)
    starts = [
        pl.multiple_of(lax.rem(y - s + 4, 4) * 256 + f, 128)
        for s, f in ((0, 0), (1, 0), (2, 0), (2, 128), (3, 0))
    ]

    @pl.loop(0, 4)
    def _(n):
        cells = pl.ds(pl.multiple_of(n * 256, 256), 256)
        total = jnp.zeros((256, 256), F32)
        for piece, first in zip(d, starts):
            total += dot(turned[:, pl.ds(first, piece.shape[0])], piece[:, cells], 1, 0)
        near[:, cells] = total


def near_terms(group, rows, d):
    call = in_vmem(
        near_kernel,
        [((256, 1024), F32)],
        [pltpu.VMEM((256, 1024), BF16)],
        2 * 256 * 1024 * 1024,
        60,
    )
    return call(group, rows, *d)[0]


def store_rows(outs, block, hot, extra, cols):
    for g in range(GROUPS):
        part = (block[g * 256 : g * 256 + 256] + hot[g] * extra).astype(BF16)
        for dc in range(2):
            for dx in range(4):
                first = dc * 128 + dx * 32
                outs[dc][dx * 64 + g * 32 : dx * 64 + g * 32 + 32, cols] = part[first : first + 32]


def start_copies(pairs, sems):
    copies = [pltpu.make_async_copy(a, b, sems.at[n]) for n, (a, b) in enumerate(pairs)]
    for copy in copies:
        copy.start()
    return copies


def operator_kernel(group, keep_ref, came, *refs):
    sources, m_refs, eta_refs = refs[:7], refs[7:9], refs[9:11]
    held, lhs, op, sems = refs[11:18], refs[18], refs[19], refs[20]
    near, right, w = held[0], held[1], held[2:]
    pairs = [(sources[0], near)]
    for n in range(4):
        rows = pl.ds(n * 256, 256)
        pairs.append((sources[1].at[rows], right.at[rows]))
    pairs += list(zip(sources[2:], w))
    copies = start_copies(pairs, sems)
    turn = offsets_matrix(lax.axis_index("x"), lax.axis_index("c"))
    pick = identity(128)[:8]

    @pl.loop(0, 4)
    def _(n):
        lanes = pl.ds(pl.multiple_of(n * 512, 512), 512)
        tiles = pl.ds(n * 16, 16)
        ids = came[tiles, 64:72, :]
        ids = jnp.concatenate([ids] * 4, axis=1).reshape(512, 128)
        ids = dot(pick, ids, 1, 1)[0:1]
        keep = keep_ref[:, lanes]
        part = dot(turn[:, :128], came[tiles, 0:32, :].reshape(512, 128), 1, 1)
        part += dot(turn[:, 128:], came[tiles, 32:64, :].reshape(512, 128), 1, 1)
        for g in range(GROUPS):
            mask = keep * (ids == g).astype(F32)
            lhs[g * 256 : g * 256 + 256, lanes] = jnp.where(mask > 0.5, part, 0.0).astype(BF16)

    hot = [jnp.where(group[0] == g, 1.0, 0.0) for g in range(GROUPS)]
    copies[0].wait()
    halves = (op.at[:256], op.at[256:])
    for n in range(4):
        copies[1 + n].wait()
        cells = slice(n * 256, n * 256 + 256)
        store_rows(halves, dot(lhs[...], right[cells, :], 1, 1), hot, near[:, cells], cells)
    outs = start_copies(list(zip(halves, m_refs)), sems.at[10:12])
    for copy in copies[5:]:
        copy.wait()
    for s, spans in ((0, (w[0],)), (1, (w[1],)), (3, (w[4],)), (2, (w[2], w[3]))):
        depth = spans[0].shape[0]
        block = dot(op[:, :depth], spans[0][...], 1, 0)
        for m, span in enumerate(spans[1:]):
            block += dot(op[:, (m + 1) * depth : (m + 2) * depth], span[...], 1, 0)
        for dc in range(2):
            eta_refs[dc][:, s * 256 : s * 256 + 256] = block[dc * 256 : dc * 256 + 256].astype(
                BF16
            )
    for copy in outs:
        copy.wait()


def operator(group, came, keep, near, right_factors, w):
    sources = (near, right_factors, *w)
    return pl.pallas_call(
        operator_kernel,
        grid_spec=pltpu.PrefetchScalarGridSpec(
            num_scalar_prefetch=1,
            grid=(),
            in_specs=[pl.BlockSpec(memory_space=pltpu.VMEM)] * 2
            + [pl.BlockSpec(memory_space=pltpu.HBM)] * len(sources),
            out_specs=[pl.BlockSpec(memory_space=pltpu.HBM)] * 2
            + [pl.BlockSpec(memory_space=pltpu.VMEM)] * 2,
            scratch_shapes=[pltpu.VMEM(v.shape, v.dtype) for v in sources]
            + [
                pltpu.VMEM((512, 2048), BF16),
                pltpu.VMEM((512, 1024), BF16),
                pltpu.SemaphoreType.DMA((12,)),
            ],
        ),
        out_shape=[jax.ShapeDtypeStruct((256, 1024), BF16)] * 4,
        compiler_params=pltpu.CompilerParams(vmem_limit_bytes=VMEM_GRANT),
        cost_estimate=pl.CostEstimate(
            flops=2 * 512 * 1024 * 3072, bytes_accessed=11 << 20, transcendentals=0
        ),
        name="operator",
    )(group, keep, came, *sources)


def gather_y(block):
    half = block.shape[0] // 2
    before = lax.ppermute(block, "y", ring(4, 1))
    after = lax.ppermute(block, "y", ring(4, -1))
    far_top = lax.ppermute(before[:half], "y", ring(4, 1))
    far_low = lax.ppermute(after[half:], "y", ring(4, -1))
    return block, before, far_top, far_low, after


def step(
    samples_w, dense_tiles, left_factors, right_factors, ranks, area_blocks, area_group, counts
):
    z, x, c, y = (lax.axis_index(a) for a in ("z", "x", "c", "y"))
    k = (z * 4 + x) * 2 + c
    d = gather_y(dense_tiles)
    sent, rows = messages(area_group, area_blocks, left_factors)
    came = exchange(sent, TILE)
    w = gather_y(samples_w)
    near = near_terms(area_group, rows, d)
    keep = (jnp.arange(32, dtype=jnp.int32)[None, :] < ranks).astype(F32).reshape(1, 2048)
    top, low, eta_keep, eta_send = operator(
        area_group, came, keep, near, right_factors, w
    )
    eta_came = lax.ppermute(eta_send, "c", ring(2, 1))
    top_before = lax.ppermute(top, "y", ring(4, 1))
    low_after = lax.ppermute(low, "y", ring(4, -1))
    top_far = lax.ppermute(top_before, "y", ring(4, 1))
    low_far = lax.ppermute(low_after, "y", ring(4, -1))
    low_before = lax.ppermute(low, "y", ring(4, 1))
    top_after = lax.ppermute(top, "y", ring(4, -1))
    core_sum = (eta_keep.astype(F32) + eta_came.astype(F32)).astype(BF16).reshape(4, 64, 1024)
    x_sum = core_sum[0].astype(F32)
    came_x = [lax.ppermute(core_sum[s], "x", ring(4, -s)) for s in (2, 1, 3)]
    for part in came_x:
        x_sum = x_sum + part.astype(F32)
    z_parts = exchange(x_sum.astype(BF16).reshape(8, 8, 1024), ("z",))
    linear = jnp.sum(z_parts.astype(F32), axis=0)
    grad = area_gradient(linear, counts.reshape(64, 4, 8)[k, y])

    pieces = grad.reshape(8, 4, 256)
    by_y = jnp.stack([at(pieces, (y - t) % 4, 1) for t in range(4)])
    got = exchange(
        jnp.broadcast_to(by_y[None], (8, 4, 8, 256)).reshape(32, 8, 256), ("z", "y")
    )
    got = got.reshape(8, 4, 8, 256)
    grad_out = at(got, z).reshape(32, 256)
    g_own = jnp.stack([at(got, (y - s) % 4, 1) for s in range(4)])
    by_x = {s: lax.ppermute(g_own, "x", ring(4, s)) for s in (2, 1, 3)}
    row = jnp.stack([g_own, by_x[1], by_x[2], by_x[3]], axis=1).reshape(1024, 256)
    other = lax.ppermute(row, "c", ring(2, 1))
    top_all = jnp.concatenate([top, top_before, top_far, top_after], axis=0)
    low_all = jnp.concatenate([low, low_before, low_far, low_after], axis=0)
    own_part = lax.optimization_barrier(dot(top_all, row, 0, 0))
    return grad_out, (own_part + dot(low_all, other, 0, 0)).astype(BF16)


def solution(mesh):
    plane = Mesh(mesh.devices.reshape(8, 4, 2, 4), ("z", "x", "c", "y"))
    return jax.shard_map(
        step,
        mesh=plane,
        in_specs=(
            P(TILE, "y"),
            P(("z", "x", "c", "y"), None),
            P(TILE, None),
            P(TILE, None),
            P(None, TILE),
            P(TILE, None),
            P(TILE),
            P(),
        ),
        out_specs=(P(TILE, "y"), P(TILE, "y")),
        check_vma=False,
    )
```

```python
import jax
import jax.numpy as jnp
from jax import lax
from jax.experimental import pallas as pl
from jax.experimental.pallas import tpu as pltpu
from jax.sharding import Mesh, PartitionSpec as P


GROUPS = 2
TILE = ("z", "x", "c")
F32 = jnp.float32
BF16 = jnp.bfloat16
VMEM_GRANT = 60 << 20


def ring(size, shift):
    return [(i, (i + shift) % size) for i in range(size)]


def dot(a, b, ca, cb):
    return lax.dot_general(a, b, (((ca,), (cb,)), ((), ())), preferred_element_type=F32)


def at(values, index, axis=0):
    return lax.dynamic_index_in_dim(values, index, axis, keepdims=False)


def area_gradient(linear, counts):
    rate = 1.0 + jax.nn.softplus(linear)
    return (jax.nn.sigmoid(linear) * (counts.astype(F32)[..., None] / rate - 1.0)).astype(BF16)


def exchange(values, axes):
    return lax.all_to_all(values, axes, split_axis=0, concat_axis=0, tiled=True)


def identity(size):
    return (
        lax.broadcasted_iota(jnp.int32, (size, size), 0)
        == lax.broadcasted_iota(jnp.int32, (size, size), 1)
    ).astype(F32).astype(BF16)


def messages_kernel(place, rows_hbm, left_hbm, out_hbm, rows_out, parts, left, out, sems):
    y = lax.axis_index("y")
    first = pltpu.make_async_copy(rows_hbm.at[:, y], parts, sems.at[0])
    first.start()
    loads = []
    for n in range(4):
        cols = pl.ds(n * 512, 512)
        loads.append(pltpu.make_async_copy(left_hbm.at[:, cols], left.at[n], sems.at[1 + n]))
        loads[n].start()
    first.wait()
    rows_out[...] = parts[...].reshape(256, 1024)
    ids = jnp.full((16, 8, 128), place[0], jnp.int32).astype(F32).astype(BF16)
    eye = identity(256)
    stores = []
    for n in range(4):
        loads[n].wait()
        part = dot(rows_out[...], left[n], 1, 0).astype(BF16)
        for half in range(2):
            block = dot(eye, part[:, half * 256 : half * 256 + 256], 1, 1).astype(BF16)
            block = block.reshape(8, 32, 256)
            tiles = slice(n * 16 + half * 8, n * 16 + half * 8 + 8)
            out[tiles, 0:32, :] = block[:, :, :128]
            out[tiles, 32:64, :] = block[:, :, 128:]
        out[n * 16 : n * 16 + 16, 64:72, :] = ids
        tiles = pl.ds(n * 16, 16)
        stores.append(pltpu.make_async_copy(out.at[tiles], out_hbm.at[tiles], sems.at[5 + n]))
        stores[n].start()
    for store in stores:
        store.wait()


def messages(place, area_blocks, left_factors):
    return pl.pallas_call(
        messages_kernel,
        grid_spec=pltpu.PrefetchScalarGridSpec(
            num_scalar_prefetch=1,
            grid=(),
            in_specs=[pl.BlockSpec(memory_space=pltpu.HBM)] * 2,
            out_specs=[
                pl.BlockSpec(memory_space=pltpu.HBM),
                pl.BlockSpec(memory_space=pltpu.VMEM),
            ],
            scratch_shapes=[
                pltpu.VMEM((32, 8, 1024), BF16),
                pltpu.VMEM((4, 1024, 512), BF16),
                pltpu.VMEM((64, 72, 128), BF16),
                pltpu.SemaphoreType.DMA((9,)),
            ],
        ),
        out_shape=[
            jax.ShapeDtypeStruct((64, 72, 128), BF16),
            jax.ShapeDtypeStruct((256, 1024), BF16),
        ],
        compiler_params=pltpu.CompilerParams(vmem_limit_bytes=VMEM_GRANT),
        cost_estimate=pl.CostEstimate(
            flops=2 * 256 * 1024 * 2048, bytes_accessed=6 << 20, transcendentals=0
        ),
        name="messages",
    )(place, area_blocks.reshape(32, 4, 8, 1024), left_factors)


def in_vmem(kernel, outs, scratch, flops, grant):
    def call(place, *values):
        size = sum(v.size * v.dtype.itemsize for v in values)
        return pl.pallas_call(
            kernel,
            grid_spec=pltpu.PrefetchScalarGridSpec(
                num_scalar_prefetch=1,
                grid=(),
                in_specs=[pl.BlockSpec(memory_space=pltpu.VMEM)] * len(values),
                out_specs=[pl.BlockSpec(memory_space=pltpu.VMEM)] * len(outs),
                scratch_shapes=scratch,
            ),
            out_shape=[jax.ShapeDtypeStruct(*out) for out in outs],
            compiler_params=pltpu.CompilerParams(vmem_limit_bytes=grant << 20),
            cost_estimate=pl.CostEstimate(flops=flops, bytes_accessed=size, transcendentals=0),
        )(place, *values)

    return call


def offsets_matrix(x, c):
    row = lax.broadcasted_iota(jnp.int32, (256, 256), 0)
    dc, dx, low, r = row >> 7, (row >> 5) & 3, (row >> 3) & 3, row & 7
    area = low * 64 + ((x - dx) & 3) * 16 + ((c + dc) & 1) * 8 + r
    return (lax.broadcasted_iota(jnp.int32, (256, 256), 1) == area).astype(F32).astype(BF16)


def near_kernel(group, rows, *refs):
    d, near, turned = refs[:5], refs[5], refs[6]
    x, c, y = (lax.axis_index(a) for a in ("x", "c", "y"))
    turned[...] = dot(offsets_matrix(x, c), rows[...], 1, 0).astype(BF16)
    starts = [
        pl.multiple_of(lax.rem(y - s + 4, 4) * 256 + f, 128)
        for s, f in ((0, 0), (1, 0), (2, 0), (2, 128), (3, 0))
    ]

    @pl.loop(0, 4)
    def _(n):
        cells = pl.ds(pl.multiple_of(n * 256, 256), 256)
        total = jnp.zeros((256, 256), F32)
        for piece, first in zip(d, starts):
            total += dot(turned[:, pl.ds(first, piece.shape[0])], piece[:, cells], 1, 0)
        near[:, cells] = total


def near_terms(group, rows, d):
    call = in_vmem(
        near_kernel,
        [((256, 1024), F32)],
        [pltpu.VMEM((256, 1024), BF16)],
        2 * 256 * 1024 * 1024,
        60,
    )
    return call(group, rows, *d)[0]


def store_rows(outs, block, hot, extra, cols):
    for g in range(GROUPS):
        part = (block[g * 256 : g * 256 + 256] + hot[g] * extra).astype(BF16)
        for dc in range(2):
            for dx in range(4):
                first = dc * 128 + dx * 32
                outs[dc][dx * 64 + g * 32 : dx * 64 + g * 32 + 32, cols] = part[first : first + 32]


def start_copies(pairs, sems):
    copies = [pltpu.make_async_copy(a, b, sems.at[n]) for n, (a, b) in enumerate(pairs)]
    for copy in copies:
        copy.start()
    return copies


def operator_kernel(group, keep_ref, came, *refs):
    sources, m_refs, eta_refs = refs[:7], refs[7:9], refs[9:11]
    held, lhs, op, sems = refs[11:18], refs[18], refs[19], refs[20]
    near, right, w = held[0], held[1], held[2:]
    pairs = [(sources[0], near)]
    for n in range(4):
        rows = pl.ds(n * 256, 256)
        pairs.append((sources[1].at[rows], right.at[rows]))
    pairs += list(zip(sources[2:], w))
    copies = start_copies(pairs, sems)
    turn = offsets_matrix(lax.axis_index("x"), lax.axis_index("c"))
    pick = identity(128)[:8]

    @pl.loop(0, 4)
    def _(n):
        lanes = pl.ds(pl.multiple_of(n * 512, 512), 512)
        tiles = pl.ds(n * 16, 16)
        ids = came[tiles, 64:72, :]
        ids = jnp.concatenate([ids] * 4, axis=1).reshape(512, 128)
        ids = dot(pick, ids, 1, 1)[0:1]
        keep = keep_ref[:, lanes]
        part = dot(turn[:, :128], came[tiles, 0:32, :].reshape(512, 128), 1, 1)
        part += dot(turn[:, 128:], came[tiles, 32:64, :].reshape(512, 128), 1, 1)
        part = part.astype(BF16)
        for g in range(GROUPS):
            mask = (keep * (ids == g).astype(F32)).astype(BF16)
            lhs[g * 256 : g * 256 + 256, lanes] = part * mask

    hot = [jnp.where(group[0] == g, 1.0, 0.0) for g in range(GROUPS)]
    copies[0].wait()
    halves = (op.at[:256], op.at[256:])
    for n in range(4):
        copies[1 + n].wait()
        cells = slice(n * 256, n * 256 + 256)
        store_rows(halves, dot(lhs[...], right[cells, :], 1, 1), hot, near[:, cells], cells)
    outs = start_copies(list(zip(halves, m_refs)), sems.at[10:12])
    for copy in copies[5:]:
        copy.wait()
    for s, spans in ((0, (w[0],)), (1, (w[1],)), (3, (w[4],)), (2, (w[2], w[3]))):
        depth = spans[0].shape[0]
        block = dot(op[:, :depth], spans[0][...], 1, 0)
        for m, span in enumerate(spans[1:]):
            block += dot(op[:, (m + 1) * depth : (m + 2) * depth], span[...], 1, 0)
        for dc in range(2):
            eta_refs[dc][:, s * 256 : s * 256 + 256] = block[dc * 256 : dc * 256 + 256].astype(
                BF16
            )
    for copy in outs:
        copy.wait()


def operator(group, came, keep, near, right_factors, w):
    sources = (near, right_factors, *w)
    return pl.pallas_call(
        operator_kernel,
        grid_spec=pltpu.PrefetchScalarGridSpec(
            num_scalar_prefetch=1,
            grid=(),
            in_specs=[pl.BlockSpec(memory_space=pltpu.VMEM)] * 2
            + [pl.BlockSpec(memory_space=pltpu.HBM)] * len(sources),
            out_specs=[pl.BlockSpec(memory_space=pltpu.HBM)] * 2
            + [pl.BlockSpec(memory_space=pltpu.VMEM)] * 2,
            scratch_shapes=[pltpu.VMEM(v.shape, v.dtype) for v in sources]
            + [
                pltpu.VMEM((512, 2048), BF16),
                pltpu.VMEM((512, 1024), BF16),
                pltpu.SemaphoreType.DMA((12,)),
            ],
        ),
        out_shape=[jax.ShapeDtypeStruct((256, 1024), BF16)] * 4,
        compiler_params=pltpu.CompilerParams(vmem_limit_bytes=50 << 20),
        cost_estimate=pl.CostEstimate(
            flops=2 * 512 * 1024 * 3072, bytes_accessed=11 << 20, transcendentals=0
        ),
        name="operator",
    )(group, keep, came, *sources)


def gather_y(block):
    half = block.shape[0] // 2
    before = lax.ppermute(block, "y", ring(4, 1))
    after = lax.ppermute(block, "y", ring(4, -1))
    far_top = lax.ppermute(before[:half], "y", ring(4, 1))
    far_low = lax.ppermute(after[half:], "y", ring(4, -1))
    return block, before, far_top, far_low, after


def step(
    samples_w, dense_tiles, left_factors, right_factors, ranks, area_blocks, area_group, counts
):
    z, x, c, y = (lax.axis_index(a) for a in ("z", "x", "c", "y"))
    k = (z * 4 + x) * 2 + c
    d = gather_y(dense_tiles)
    sent, rows = messages(area_group, area_blocks, left_factors)
    came = exchange(sent, TILE)
    w = gather_y(samples_w)
    near = near_terms(area_group, rows, d)
    keep = (jnp.arange(32, dtype=jnp.int32)[None, :] < ranks).astype(F32).reshape(1, 2048)
    top, low, eta_keep, eta_send = operator(
        area_group, came, keep, near, right_factors, w
    )
    eta_came = lax.ppermute(eta_send, "c", ring(2, 1))
    top_before = lax.ppermute(top, "y", ring(4, 1))
    low_after = lax.ppermute(low, "y", ring(4, -1))
    top_far = lax.ppermute(top_before, "y", ring(4, 1))
    low_far = lax.ppermute(low_after, "y", ring(4, -1))
    low_before = lax.ppermute(low, "y", ring(4, 1))
    top_after = lax.ppermute(top, "y", ring(4, -1))
    core_sum = (eta_keep.astype(F32) + eta_came.astype(F32)).astype(BF16).reshape(4, 64, 1024)
    x_sum = core_sum[0].astype(F32)
    came_x = [lax.ppermute(core_sum[s], "x", ring(4, -s)) for s in (2, 1, 3)]
    for part in came_x:
        x_sum = x_sum + part.astype(F32)
    z_parts = exchange(x_sum.astype(BF16).reshape(8, 8, 1024), ("z",))
    linear = jnp.sum(z_parts.astype(F32), axis=0)
    grad = area_gradient(linear, counts.reshape(64, 4, 8)[k, y])

    pieces = grad.reshape(8, 4, 256)
    by_y = jnp.stack([at(pieces, (y - t) % 4, 1) for t in range(4)])
    got = exchange(jnp.broadcast_to(by_y[:, None], (4, 8, 8, 256)).reshape(32, 8, 256), ("y", "z"))
    got = got.reshape(4, 8, 8, 256)
    g_own = jnp.stack([at(got, (y - s) % 4) for s in range(4)])
    by_x = {s: lax.ppermute(g_own, "x", ring(4, s)) for s in (2, 1, 3)}
    grad_out = at(got, z, 1).reshape(32, 256)
    row = jnp.stack([g_own, by_x[1], by_x[2], by_x[3]], axis=1).reshape(1024, 256)
    other = lax.ppermute(row, "c", ring(2, 1))
    top_all = jnp.concatenate([top, top_before, top_far, top_after], axis=0)
    low_all = jnp.concatenate([low, low_before, low_far, low_after], axis=0)
    own_part = lax.optimization_barrier(dot(top_all, row, 0, 0))
    return grad_out, (own_part + dot(low_all, other, 0, 0)).astype(BF16)


def solution(mesh):
    plane = Mesh(mesh.devices.reshape(8, 4, 2, 4), ("z", "x", "c", "y"))
    return jax.shard_map(
        step,
        mesh=plane,
        in_specs=(
            P(TILE, "y"),
            P(("z", "x", "c", "y"), None),
            P(TILE, None),
            P(TILE, None),
            P(None, TILE),
            P(TILE, None),
            P(TILE),
            P(),
        ),
        out_specs=(P(TILE, "y"), P(TILE, "y")),
        check_vma=False,
    )
```
